1024 devices in a mesh: kv: 8 (over y), key: 16 (over z), tok: 8 (over x, core).
Axes of the slice: x: 4, y: 8, z: 16, core: 2. Of those that a mesh axis runs over, the one named last changes fastest.
Arguments:
- queries: bfloat16 [4096, 8192], P('key', ('kv', 'tok')), may hold values from -200 to 200
- keys: bfloat16 [4096, 1024], P('key', 'kv'), may hold values from -8 to 8
- values: bfloat16 [4096, 1024], P('key', 'kv'), may hold values from -6 to 6
- doc_ids: int32 [4096], replicated, may hold values from 0 to 5, never falling along the last dimension, each value on 1 to 2048 neighbouring positions
- out_weight: bfloat16 [8192, 8192], P('kv', 'tok'), may hold values from -0.0625 to 0.0625
Outputs:
- mixed: bfloat16 [4096, 8192], P(('key', 'kv'), 'tok')
The draws below stay inside these ranges and needn't reach their ends.
Inputs may be any that keep to these rules, and one draw needn't show every extreme that they name: `doc_ids`: document numbers never fall along the window; a document covers at most 2048 positions and some document covers exactly that many.
All inputs are finite; a program needn't handle non-finite values.
Results may differ from the reference program's by a relative error of at most 0.014.
Values may be sent and summed in bfloat16 or wider, within the bound.
No kernel may reach another device: no remote copies, remote signals or barrier semaphores. Data moves between devices by JAX's collectives and lax.ppermute only.
A program may use at most 32 MiB of HBM per device.

```python
import math
import jax
import jax.numpy as jnp
import numpy as np
from jax import lax

D = 8192
QUERY_HEADS = 64
KEY_VALUE_HEADS = 8
HEAD_SIZE = 128
TOK_DEV = 256
REACH = 8
WINDOW_TOKENS = 4096
N_KEY = 16


def closing_keys(key):
    sampled_rows = jnp.clip(jax.random.normal(jax.random.fold_in(key, 11), (WINDOW_TOKENS, KEY_VALUE_HEADS * HEAD_SIZE), jnp.float32), -6.0, 6.0)
    return sampled_rows


def draw_keys(key, part):
    return closing_keys(key).astype(jnp.bfloat16)


def draw_queries(key, part):
    sampled_rows = 2.5 * jnp.clip(jax.random.normal(jax.random.fold_in(key, 21), (WINDOW_TOKENS, QUERY_HEADS * HEAD_SIZE), jnp.float32), -6.0, 6.0)
    return sampled_rows.astype(jnp.bfloat16)


def block_levels(rng, dims, cuts, low, high):
    level, own = 1.0, jax.random.fold_in(rng, 6)
    for dim, blocks in cuts:
        steps = jnp.exp(jax.random.uniform(jax.random.fold_in(own, dim), (blocks,), jnp.float32, low / len(cuts), high / len(cuts)))
        level = level * jnp.repeat(steps, dims[dim] // blocks).reshape([-1 if axis == dim else 1 for axis in range(len(dims))])
    return level


def length_profile(count, total, bound, lean):
    loads = [(1 << 20) // math.isqrt(standing ** lean) + 1 for standing in range(2, count + 1)]
    surplus, holding = total - bound - (count - 1), [1] * (count - 1)
    while surplus > 0:
        movable = [i for i in range(count - 1) if holding[i] < bound]
        pool, budget = sum([loads[i] for i in movable]), surplus
        for i in movable:
            addition = min(bound - holding[i], max(1, budget * loads[i] // pool), surplus)
            holding[i] = holding[i] + addition
            surplus = surplus - addition
    return np.array([bound] + holding)


def uneven_parts(key, count, total, bound, slope):
    if count == 2:
        one = jax.random.randint(key, (), max(1, total - bound), min(bound, total - 1) + 1)
        return jnp.stack([one, total - one])
    sizes = jnp.asarray(length_profile(count, total, bound, slope), jnp.int32)
    pairs = (count - 1) // 2
    giver, receiver = sizes[1:1 + 2 * pairs:2], sizes[2:2 + 2 * pairs:2]
    room = jnp.minimum(giver - 1, bound - receiver)
    shifted = jax.random.randint(jax.random.fold_in(key, 1), (pairs,), 0, 1 << 20) % (room + 1)
    sizes = sizes.at[1:1 + 2 * pairs:2].set(giver - shifted).at[2:2 + 2 * pairs:2].set(receiver + shifted)
    return sizes[jax.random.permutation(jax.random.fold_in(key, 2), count)]


def noise(key, dims, spread, reach, split=(), kind=jnp.bfloat16):
    level = block_levels(key, dims, split, -0.22, 0.18) if split else 1.0
    result = jax.random.normal(key, dims, jnp.float32) * spread * level
    return jnp.minimum(jnp.maximum(result, -reach), reach).astype(kind)


def setup_inputs(seed: int = 0) -> dict:
    arg_keys = jax.random.split(jax.random.key(seed), 6)
    queries = draw_queries(jax.random.fold_in(arg_keys[5], 71), 0)
    keys = draw_keys(jax.random.fold_in(arg_keys[5], 71), 0)
    values = noise(arg_keys[2], (WINDOW_TOKENS, KEY_VALUE_HEADS * HEAD_SIZE), 1.0, 6.0, ((0, 16), (1, 8)))
    doc_ids = jnp.searchsorted(jnp.cumsum(uneven_parts(arg_keys[3], 6, WINDOW_TOKENS, REACH * TOK_DEV, 2)), jnp.arange(WINDOW_TOKENS), side="right").astype(jnp.int32)
    out_weight = noise(arg_keys[4], (QUERY_HEADS * HEAD_SIZE, D), (QUERY_HEADS * HEAD_SIZE) ** -0.5, 0.0625, ((0, 8), (1, 8)))
    return {"queries": queries, "keys": keys, "values": values, "doc_ids": doc_ids, "out_weight": out_weight}


very_low = -1e+30

def partial_block(query_block, key_block, value_block, query_docs, key_docs, query_pos, key_pos):
    group_width = QUERY_HEADS // KEY_VALUE_HEADS
    key_wide = jnp.repeat(key_block, group_width, axis=1).astype(jnp.float32)
    value_wide = jnp.repeat(value_block, group_width, axis=1).astype(jnp.float32)
    scores = jnp.einsum('qhd,shd->hqs', query_block.astype(jnp.float32), key_wide) * (1.0 / math.sqrt(HEAD_SIZE))
    allowed = (query_docs[:, None] == key_docs[None, :]) & (key_pos[None, :] <= query_pos[:, None])
    highest = lax.optimization_barrier(jnp.max(jnp.where(allowed[None], scores, very_low), axis=2))
    weights = jnp.exp(jnp.where(allowed[None], scores - highest[:, :, None], very_low))
    totals = lax.optimization_barrier(jnp.sum(weights, axis=2)).T
    probs = weights.astype(jnp.bfloat16)
    weighted = jnp.einsum('hqs,shd->qhd', probs.astype(jnp.float32), value_wide)
    positive = totals > 0
    safe = jnp.where(positive, totals, 1.0)
    piece = (weighted / safe[:, :, None]).astype(jnp.bfloat16)
    log_total = jnp.where(positive, highest.T + jnp.log(safe), very_low)
    return (piece, log_total)

def reference(queries, keys, values, doc_ids, out_weight):
    query_three = queries.reshape(WINDOW_TOKENS, QUERY_HEADS, HEAD_SIZE)
    key_cube = keys.reshape(WINDOW_TOKENS, KEY_VALUE_HEADS, HEAD_SIZE)
    value_cube = values.reshape(WINDOW_TOKENS, KEY_VALUE_HEADS, HEAD_SIZE)
    positions = jnp.arange(WINDOW_TOKENS, dtype=jnp.int32)
    outputs = []
    for query_range in range(N_KEY):
        first_query = query_range * TOK_DEV
        query_block = query_three[first_query:first_query + TOK_DEV]
        piece_list = []
        total_list = []
        for offset in range(min(REACH, query_range) + 1):
            first_key = (query_range - offset) * TOK_DEV
            piece, log_total = partial_block(query_block, key_cube[first_key:first_key + TOK_DEV], value_cube[first_key:first_key + TOK_DEV], doc_ids[first_query:first_query + TOK_DEV], doc_ids[first_key:first_key + TOK_DEV], positions[first_query:first_query + TOK_DEV], positions[first_key:first_key + TOK_DEV])
            piece_list.append(piece)
            total_list.append(log_total)
        pieces = jnp.stack(piece_list)
        log_totals = jnp.stack(total_list)
        top = lax.optimization_barrier(jnp.max(log_totals, axis=0))
        factors = jnp.exp(log_totals - top[None])
        numerator = lax.optimization_barrier(jnp.sum(factors[..., None] * pieces.astype(jnp.float32), axis=0))
        denominator = lax.optimization_barrier(jnp.sum(factors, axis=0))
        outputs.append((numerator / denominator[..., None]).astype(jnp.bfloat16))
    attn = jnp.concatenate(outputs, axis=0).reshape(WINDOW_TOKENS, QUERY_HEADS * HEAD_SIZE)
    return jnp.dot(attn, out_weight, preferred_element_type=jnp.float32).astype(jnp.bfloat16)
```

```python
import math

import jax
import jax.numpy as jnp
from jax import lax
from jax.experimental import pallas as pl
from jax.experimental.pallas import tpu as pltpu
from jax.sharding import PartitionSpec as P

HEAD_SIZE = 128
REACH = 8
LOW = -1e30
EXTRA = 16


def dot(a, b, contract):
    return lax.dot_general(a, b, (contract, ((), ())), preferred_element_type=jnp.float32)


def attend_kernel(range_ref, bounds_ref, queries_ref, pairs_ref, out_ref, key_buf, value_buf, bias):
    own = range_ref[0]
    slice_rows = pairs_ref.shape[1]
    range_count = pairs_ref.shape[0]
    head_count = queries_ref.shape[0]
    query_count = queries_ref.shape[1]
    first = bounds_ref[0:1, :]
    last = bounds_ref[1:2, :]
    for back in range(REACH + 1):
        source = lax.rem(own - back + range_count, range_count)
        pair = pairs_ref[source]
        rows = pl.ds(back * slice_rows, slice_rows)
        key_buf[rows, :] = pair[:, :HEAD_SIZE]
        value_buf[rows, :] = pair[:, HEAD_SIZE:]
        place = lax.broadcasted_iota(jnp.int32, (slice_rows, query_count), 0) - back * query_count
        allowed = place >= first
        if back == 0:
            allowed = allowed & (place <= last)
        bias[rows, :] = jnp.where(allowed, 0.0, LOW)
    factor = math.log2(math.e) / math.sqrt(HEAD_SIZE)
    row = lax.broadcasted_iota(jnp.int32, (EXTRA, query_count), 0)
    for head in range(head_count):
        scores = dot(key_buf[...], queries_ref[head], ((1,), (1,))) * factor + bias[...]
        highest = jnp.maximum(jnp.max(scores, axis=0, keepdims=True), 0.1 * LOW)
        weights = jnp.exp2(scores - highest)
        total = jnp.sum(weights, axis=0, keepdims=True)
        weighted = dot(value_buf[...], weights.astype(jnp.bfloat16), ((0,), (0,)))
        positive = total > 0
        safe = jnp.where(positive, total, 1.0)
        out_ref[head, :HEAD_SIZE, :] = (weighted * (1.0 / safe)).astype(jnp.bfloat16)
        log_total = jnp.where(positive, highest + jnp.log2(safe), LOW)
        one = log_total.astype(jnp.bfloat16).astype(jnp.float32)
        rest = log_total - one
        two = rest.astype(jnp.bfloat16).astype(jnp.float32)
        three = rest - two
        packed = jnp.where(
            row == 0, one, jnp.where(row == 1, two, jnp.where(row == 2, three, 0.0))
        )
        out_ref[head, HEAD_SIZE:, :] = packed.astype(jnp.bfloat16)


def attend(range_index, bounds, queries, pairs):
    head_count, query_count, _ = queries.shape
    key_count = (REACH + 1) * pairs.shape[1]
    vmem = pl.BlockSpec(memory_space=pltpu.VMEM)
    return pl.pallas_call(
        attend_kernel,
        out_shape=jax.ShapeDtypeStruct(
            (head_count, HEAD_SIZE + EXTRA, query_count), jnp.bfloat16
        ),
        in_specs=[pl.BlockSpec(memory_space=pltpu.SMEM), vmem, vmem, vmem],
        out_specs=vmem,
        scratch_shapes=[
            pltpu.VMEM((key_count, HEAD_SIZE), jnp.bfloat16),
            pltpu.VMEM((key_count, HEAD_SIZE), jnp.bfloat16),
            pltpu.VMEM((key_count, query_count), jnp.float32),
        ],
        compiler_params=pltpu.CompilerParams(vmem_limit_bytes=16 << 20),
        name="attend",
    )(range_index, bounds, queries, pairs)


def merge_kernel(parts_ref, out_ref):
    count = parts_ref.shape[0]
    logs = []
    for source in range(count):
        extra = parts_ref[source, HEAD_SIZE:, :].astype(jnp.float32)
        logs.append((extra[2:3] + extra[1:2]) + extra[0:1])
    top = logs[0]
    for log in logs[1:]:
        top = jnp.maximum(top, log)
    numerator, denominator = 0.0, 0.0
    for source in range(count):
        weight = jnp.exp2(logs[source] - top)
        denominator = denominator + weight
        numerator = numerator + weight * parts_ref[source, :HEAD_SIZE, :].astype(jnp.float32)
    merged = (numerator * (1.0 / denominator)).astype(jnp.bfloat16)
    for target in range(count):
        out_ref[target] = merged


def merge(parts):
    count, _, query_count = parts.shape
    vmem = pl.BlockSpec(memory_space=pltpu.VMEM)
    return pl.pallas_call(
        merge_kernel,
        out_shape=jax.ShapeDtypeStruct((count, HEAD_SIZE, query_count), jnp.bfloat16),
        in_specs=[vmem],
        out_specs=vmem,
        compiler_params=pltpu.CompilerParams(vmem_limit_bytes=16 << 20),
        name="merge",
    )(parts)


def exchange(x, axis):
    return lax.all_to_all(x, axis, 0, 0, tiled=True)


def spread(x, axis):
    return exchange(jnp.broadcast_to(x[None], (lax.axis_size(axis),) + x.shape), axis)


def per_device(queries, keys, values, doc_ids, out_weight):
    key_index = lax.axis_index("key")
    tok_index = lax.axis_index("tok")
    tok_count = lax.axis_size("tok")
    kv_count = lax.axis_size("kv")
    row_count = queries.shape[0]
    slice_rows = row_count // tok_count
    own_start = key_index * row_count
    pairs = jnp.concatenate(
        [
            lax.dynamic_slice_in_dim(keys, tok_index * slice_rows, slice_rows, 0),
            lax.dynamic_slice_in_dim(values, tok_index * slice_rows, slice_rows, 0),
        ],
        axis=1,
    )
    pairs = spread(pairs, "key")
    all_queries = lax.all_gather(queries, "tok", axis=0)
    query_docs = lax.dynamic_slice_in_dim(doc_ids, own_start, row_count)
    first = jnp.sum((doc_ids[:, None] < query_docs[None, :]).astype(jnp.int32), axis=0)
    shift = own_start + tok_index * slice_rows
    bounds = jnp.stack([first - shift, jnp.arange(row_count, dtype=jnp.int32) + own_start - shift])
    parts = attend(key_index.reshape(1), bounds, all_queries, pairs)
    merged = merge(exchange(parts, "tok"))
    attn = exchange(merged, "tok").reshape(tok_count * HEAD_SIZE, row_count)
    total = jnp.einsum("kq,kn->qn", attn, out_weight, preferred_element_type=jnp.float32)
    total = total.astype(jnp.bfloat16).reshape(kv_count, row_count // kv_count, -1)
    shares = exchange(total, "kv")
    return jnp.sum(shares.astype(jnp.float32), axis=0).astype(jnp.bfloat16)


def solution(mesh):
    placed = (P("key", ("kv", "tok")), P("key", "kv"), P("key", "kv"), P(), P("kv", "tok"))
    return jax.shard_map(
        per_device, mesh=mesh, in_specs=placed, out_specs=P(("key", "kv"), "tok"), check_vma=False
    )
```

```python
import math

import jax
import jax.numpy as jnp
from jax import lax
from jax.experimental import pallas as pl
from jax.experimental.pallas import tpu as pltpu
from jax.sharding import PartitionSpec as P


HEAD_SIZE = 128
REACH = 8
LOW = -1e30
EXTRA = 16
MOST_DOC = 5
LANES = 128
CORES = 2
FACTOR = math.log2(math.e) / math.sqrt(HEAD_SIZE)

VMEM = pl.BlockSpec(memory_space=pltpu.VMEM)
SMEM = pl.BlockSpec(memory_space=pltpu.SMEM)


def dot(a, b, contract):
    return lax.dot_general(a, b, (contract, ((), ())), preferred_element_type=jnp.float32)


def first_kernel(index_ref, docs_ref, first_ref):
    query_count = first_ref.shape[1]
    per_range = query_count // LANES
    docs = docs_ref[...]
    own = index_ref[0] * per_range
    query_docs = jnp.concatenate(
        [docs_ref[pl.ds(own + piece, 1), :] for piece in range(per_range)], axis=1
    )
    first = jnp.zeros((1, query_count), jnp.float32)
    for number in range(1, MOST_DOC + 1):
        smaller = jnp.where(docs < number, 1.0, 0.0)
        begins = jnp.sum(jnp.sum(smaller, axis=0, keepdims=True), axis=1, keepdims=True)
        first = jnp.where(query_docs == number, begins, first)
    first_ref[...] = first


def find_first(index, docs, query_count):
    return pl.pallas_call(
        first_kernel,
        out_shape=jax.ShapeDtypeStruct((1, query_count), jnp.float32),
        in_specs=[SMEM, VMEM],
        out_specs=VMEM,
        compiler_params=pltpu.CompilerParams(vmem_limit_bytes=4 << 20),
        name="first",
    )(index, docs)


def load_slice(own, tok, first_ref, pairs_ref, key_buf, value_buf, bias):
    range_count, slice_rows, _ = pairs_ref.shape
    query_count = first_ref.shape[1]
    first = first_ref[...] - (own * query_count + tok * slice_rows).astype(jnp.float32)
    last = lax.broadcasted_iota(jnp.int32, (1, query_count), 1) - tok * slice_rows
    for back in range(REACH + 1):
        source = lax.rem(own - back + range_count, range_count)
        pair = pairs_ref[source]
        rows = pl.ds(back * slice_rows, slice_rows)
        key_buf[rows, :] = pair[:, :HEAD_SIZE]
        value_buf[rows, :] = pair[:, HEAD_SIZE:]
        place = lax.broadcasted_iota(jnp.int32, (slice_rows, query_count), 0) - back * query_count
        allowed = place.astype(jnp.float32) >= first
        if back == 0:
            allowed = allowed & (place <= last)
        bias[rows, :] = jnp.where(allowed, 0.0, LOW)


def attend_slice(queries, key_buf, value_buf, bias):
    scores = dot(key_buf[...], queries, ((1,), (1,))) * FACTOR + bias[...]
    highest = jnp.maximum(jnp.max(scores, axis=0, keepdims=True), 0.1 * LOW)
    weights = jnp.exp2(scores - highest)
    total = jnp.sum(weights, axis=0, keepdims=True)
    weighted = dot(value_buf[...], weights.astype(jnp.bfloat16), ((0,), (0,)))
    return highest, total, weighted


def near_kernel(
    index_ref, first_ref, queries_ref, pairs_ref, stats_ref, sums_ref, key_buf, value_buf, bias
):
    load_slice(index_ref[0], index_ref[1], first_ref, pairs_ref, key_buf, value_buf, bias)
    for head in range(queries_ref.shape[0]):
        highest, total, weighted = attend_slice(queries_ref[head], key_buf, value_buf, bias)
        stats_ref[head, 0:1, :] = highest
        stats_ref[head, 1:2, :] = total
        sums_ref[head] = weighted


def far_kernel(
    index_ref,
    first_ref,
    queries_ref,
    pairs_ref,
    stats_ref,
    sums_ref,
    out_ref,
    key_buf,
    value_buf,
    bias,
):
    other = 1 - 2 * lax.rem(index_ref[1], CORES) + index_ref[1]
    load_slice(index_ref[0], other, first_ref, pairs_ref, key_buf, value_buf, bias)
    row = lax.broadcasted_iota(jnp.int32, (EXTRA, first_ref.shape[1]), 0)
    for head in range(queries_ref.shape[0]):
        highest, total, weighted = attend_slice(queries_ref[head], key_buf, value_buf, bias)
        before = stats_ref[head, 0:1, :]
        top = jnp.maximum(before, highest)
        keep, add = jnp.exp2(before - top), jnp.exp2(highest - top)
        total = keep * stats_ref[head, 1:2, :] + add * total
        positive = total > 0
        safe = jnp.where(positive, total, 1.0)
        scale = 1.0 / safe
        out_ref[head, :HEAD_SIZE, :] = (
            (keep * scale) * sums_ref[head] + (add * scale) * weighted
        ).astype(jnp.bfloat16)
        log_total = jnp.where(positive, top + jnp.log2(safe), LOW)
        one = log_total.astype(jnp.bfloat16).astype(jnp.float32)
        rest = log_total - one
        two = rest.astype(jnp.bfloat16).astype(jnp.float32)
        three = rest - two
        packed = jnp.where(
            row == 0, one, jnp.where(row == 1, two, jnp.where(row == 2, three, 0.0))
        )
        out_ref[head, HEAD_SIZE:, :] = packed.astype(jnp.bfloat16)


def buffers(pairs, query_count):
    key_count = (REACH + 1) * pairs.shape[1]
    return [
        pltpu.VMEM((key_count, HEAD_SIZE), jnp.bfloat16),
        pltpu.VMEM((key_count, HEAD_SIZE), jnp.bfloat16),
        pltpu.VMEM((key_count, query_count), jnp.float32),
    ]


def cost(queries, pairs):
    scores = queries.shape[0] * queries.shape[1] * (REACH + 1) * pairs.shape[1]
    return pl.CostEstimate(
        flops=4 * HEAD_SIZE * scores, transcendentals=scores, bytes_accessed=2 << 20
    )


def attend_near(index, first, queries, pairs):
    head_count, query_count, _ = queries.shape
    return pl.pallas_call(
        near_kernel,
        out_shape=[
            jax.ShapeDtypeStruct((head_count, 8, query_count), jnp.float32),
            jax.ShapeDtypeStruct((head_count, HEAD_SIZE, query_count), jnp.float32),
        ],
        in_specs=[SMEM, VMEM, VMEM, VMEM],
        out_specs=[VMEM, VMEM],
        scratch_shapes=buffers(pairs, query_count),
        compiler_params=pltpu.CompilerParams(vmem_limit_bytes=8 << 20),
        cost_estimate=cost(queries, pairs),
        name="near",
    )(index, first, queries, pairs)


def attend_far(index, first, queries, pairs, stats, sums):
    head_count, query_count, _ = queries.shape
    return pl.pallas_call(
        far_kernel,
        out_shape=jax.ShapeDtypeStruct(
            (head_count, HEAD_SIZE + EXTRA, query_count), jnp.bfloat16
        ),
        in_specs=[SMEM, VMEM, VMEM, VMEM, VMEM, VMEM],
        out_specs=VMEM,
        scratch_shapes=buffers(pairs, query_count),
        compiler_params=pltpu.CompilerParams(vmem_limit_bytes=8 << 20),
        cost_estimate=cost(queries, pairs),
        name="far",
    )(index, first, queries, pairs, stats, sums)


def merge_kernel(parts_ref, out_ref):
    count = parts_ref.shape[0]
    logs = []
    for source in range(count):
        extra = parts_ref[source, HEAD_SIZE:, :].astype(jnp.float32)
        logs.append((extra[2:3] + extra[1:2]) + extra[0:1])
    top = logs[0]
    for log in logs[1:]:
        top = jnp.maximum(top, log)
    numerator, denominator = 0.0, 0.0
    for source in range(count):
        weight = jnp.exp2(logs[source] - top)
        denominator = denominator + weight
        numerator = numerator + weight * parts_ref[source, :HEAD_SIZE, :].astype(jnp.float32)
    merged = (numerator * (1.0 / denominator)).astype(jnp.bfloat16)
    for target in range(count):
        out_ref[target] = merged


def merge(parts):
    count, _, query_count = parts.shape
    return pl.pallas_call(
        merge_kernel,
        out_shape=jax.ShapeDtypeStruct((count, HEAD_SIZE, query_count), jnp.bfloat16),
        in_specs=[VMEM],
        out_specs=VMEM,
        compiler_params=pltpu.CompilerParams(vmem_limit_bytes=16 << 20),
        name="merge",
    )(parts)


def arrange_kernel(index_ref, own_ref, other_ref, out_ref):
    core = lax.rem(index_ref[1], CORES)
    for chip in range(own_ref.shape[0]):
        for heads, place in ((own_ref, core), (other_ref, 1 - core)):
            row = pl.multiple_of((chip * CORES + place) * HEAD_SIZE, HEAD_SIZE)
            out_ref[pl.ds(row, HEAD_SIZE), :] = heads[chip]


def arrange(index, own, other):
    chips, _, query_count = own.shape
    return pl.pallas_call(
        arrange_kernel,
        out_shape=jax.ShapeDtypeStruct((chips * CORES * HEAD_SIZE, query_count), jnp.bfloat16),
        in_specs=[SMEM, VMEM, VMEM],
        out_specs=VMEM,
        compiler_params=pltpu.CompilerParams(vmem_limit_bytes=4 << 20),
        name="arrange",
    )(index, own, other)


def exchange(x, axis, groups=None):
    return lax.all_to_all(x, axis, 0, 0, tiled=True, axis_index_groups=groups)


def swap(x, count):
    return lax.ppermute(x, "tok", [(i, i ^ 1) for i in range(count)])


def per_device(queries, keys, values, doc_ids, out_weight):
    key_index = lax.axis_index("key")
    tok_index = lax.axis_index("tok")
    key_count = lax.axis_size("key")
    tok_count = lax.axis_size("tok")
    kv_count = lax.axis_size("kv")
    chips = tok_count // CORES
    groups = [[chip * CORES + c for chip in range(chips)] for c in range(CORES)]
    row_count = queries.shape[0]
    slice_rows = row_count // tok_count
    index = jnp.stack([key_index, tok_index])
    pair = jnp.concatenate(
        [
            lax.dynamic_slice_in_dim(keys, tok_index * slice_rows, slice_rows, 0),
            lax.dynamic_slice_in_dim(values, tok_index * slice_rows, slice_rows, 0),
        ],
        axis=1,
    )
    pairs = exchange(jnp.broadcast_to(pair[None], (key_count,) + pair.shape), "key")
    head_queries = lax.all_gather(queries, "tok", axis=0, axis_index_groups=groups)
    first = find_first(index, doc_ids.reshape(-1, LANES), row_count)
    other_pairs = swap(pairs, tok_count)
    stats, sums = attend_near(index, first, head_queries, pairs)
    parts = attend_far(index, first, head_queries, other_pairs, stats, sums)
    merged = merge(exchange(parts, "tok", groups))
    attn = exchange(merged, "tok", groups)
    other_attn = swap(attn, tok_count)
    attn = arrange(index, attn, other_attn)
    total = jnp.einsum("kq,kn->qn", attn, out_weight, preferred_element_type=jnp.float32)
    total = total.astype(jnp.bfloat16).reshape(kv_count, row_count // kv_count, -1)
    shares = exchange(total, "kv")
    return jnp.sum(shares.astype(jnp.float32), axis=0).astype(jnp.bfloat16)


def solution(mesh):
    placed = (P("key", ("kv", "tok")), P("key", "kv"), P("key", "kv"), P(), P("kv", "tok"))
    return jax.shard_map(
        per_device, mesh=mesh, in_specs=placed, out_specs=P(("key", "kv"), "tok"), check_vma=False
    )
```

```python
import math

import jax
import jax.numpy as jnp
from jax import lax
from jax.experimental import pallas as pl
from jax.experimental.pallas import tpu as pltpu
from jax.sharding import PartitionSpec as P


HEAD_SIZE = 128
REACH = 8
LOW = -1e30
EXTRA = 16
MOST_DOC = 5
LANES = 128
PAIR = 2
FACTOR = math.log2(math.e) / math.sqrt(HEAD_SIZE)

VMEM = pl.BlockSpec(memory_space=pltpu.VMEM)
SMEM = pl.BlockSpec(memory_space=pltpu.SMEM)


def dot(a, b, contract):
    return lax.dot_general(a, b, (contract, ((), ())), preferred_element_type=jnp.float32)


def query_places(query_count, target_count):
    lane = lax.broadcasted_iota(jnp.int32, (1, query_count), 1)
    half_count = query_count // PAIR
    rows = half_count // target_count
    half, rest = lane // half_count, lane % half_count
    return (rest // rows) * (rows * PAIR) + half * rows + rest % rows


def first_kernel(target_count, index_ref, docs_ref, first_ref):
    query_count = first_ref.shape[1]
    docs = docs_ref[...]
    place = query_places(query_count, target_count) + index_ref[0] * query_count
    place = place.astype(jnp.float32)
    first = jnp.zeros((1, query_count), jnp.float32)
    for number in range(1, MOST_DOC + 1):
        smaller = jnp.where(docs < number, 1.0, 0.0)
        begins = jnp.sum(jnp.sum(smaller, axis=0, keepdims=True), axis=1, keepdims=True)
        first = jnp.where(begins <= place, jnp.maximum(first, begins), first)
    first_ref[...] = first


def find_first(index, docs, query_count, target_count):
    return pl.pallas_call(
        lambda *refs: first_kernel(target_count, *refs),
        out_shape=jax.ShapeDtypeStruct((1, query_count), jnp.float32),
        in_specs=[SMEM, VMEM],
        out_specs=VMEM,
        compiler_params=pltpu.CompilerParams(vmem_limit_bytes=4 << 20),
        name="first",
    )(index, docs)


def attend_kernel(
    target_count,
    index_ref,
    first_ref,
    queries_ref,
    pairs_ref,
    out_ref,
    key_buf,
    value_buf,
    bias,
):
    own, tok = index_ref[0], index_ref[1]
    range_count, slice_rows, _ = pairs_ref.shape
    head_count, query_count, _ = queries_ref.shape
    first = first_ref[...] - (own * query_count + tok * slice_rows).astype(jnp.float32)
    last = query_places(query_count, target_count) - tok * slice_rows
    for back in range(REACH + 1):
        source = lax.rem(own - back + range_count, range_count)
        pair = pairs_ref[source]
        rows = pl.ds(back * slice_rows, slice_rows)
        key_buf[rows, :] = pair[:, :HEAD_SIZE]
        value_buf[rows, :] = pair[:, HEAD_SIZE:]
        place = lax.broadcasted_iota(jnp.int32, (slice_rows, query_count), 0) - back * query_count
        allowed = place.astype(jnp.float32) >= first
        if back == 0:
            allowed = allowed & (place <= last)
        bias[rows, :] = jnp.where(allowed, 0.0, LOW)
    row = lax.broadcasted_iota(jnp.int32, (EXTRA, query_count), 0)
    part = query_count // PAIR // target_count
    for head in range(head_count):
        queries = jnp.concatenate(
            [
                queries_ref[head, pl.ds((target * PAIR + half) * part, part), :]
                for half in range(PAIR)
                for target in range(target_count)
            ],
            axis=0,
        )
        scores = dot(key_buf[...], queries, ((1,), (1,))) * FACTOR + bias[...]
        highest = jnp.maximum(jnp.max(scores, axis=0, keepdims=True), 0.1 * LOW)
        weights = jnp.exp2(scores - highest)
        total = jnp.sum(weights, axis=0, keepdims=True)
        weighted = dot(value_buf[...], weights.astype(jnp.bfloat16), ((0,), (0,)))
        positive = total > 0
        safe = jnp.where(positive, total, 1.0)
        out_ref[head, :HEAD_SIZE, :] = (weighted * (1.0 / safe)).astype(jnp.bfloat16)
        log_total = jnp.where(positive, highest + jnp.log2(safe), LOW)
        one = log_total.astype(jnp.bfloat16).astype(jnp.float32)
        rest = log_total - one
        two = rest.astype(jnp.bfloat16).astype(jnp.float32)
        three = rest - two
        packed = jnp.where(
            row == 0, one, jnp.where(row == 1, two, jnp.where(row == 2, three, 0.0))
        )
        out_ref[head, HEAD_SIZE:, :] = packed.astype(jnp.bfloat16)


def attend(index, first, queries, pairs, target_count):
    head_count, query_count, _ = queries.shape
    key_count = (REACH + 1) * pairs.shape[1]
    return pl.pallas_call(
        lambda *refs: attend_kernel(target_count, *refs),
        out_shape=jax.ShapeDtypeStruct(
            (head_count, HEAD_SIZE + EXTRA, query_count), jnp.bfloat16
        ),
        in_specs=[SMEM, VMEM, VMEM, VMEM],
        out_specs=VMEM,
        scratch_shapes=[
            pltpu.VMEM((key_count, HEAD_SIZE), jnp.bfloat16),
            pltpu.VMEM((key_count, HEAD_SIZE), jnp.bfloat16),
            pltpu.VMEM((key_count, query_count), jnp.float32),
        ],
        compiler_params=pltpu.CompilerParams(vmem_limit_bytes=8 << 20),
        name="attend",
    )(index, first, queries, pairs)


def merge_kernel(parts_ref, out_ref):
    count = parts_ref.shape[0]
    logs = []
    for source in range(count):
        extra = parts_ref[source, HEAD_SIZE:, :].astype(jnp.float32)
        logs.append((extra[2:3] + extra[1:2]) + extra[0:1])
    top = logs[0]
    for log in logs[1:]:
        top = jnp.maximum(top, log)
    numerator, denominator = 0.0, 0.0
    for source in range(count):
        weight = jnp.exp2(logs[source] - top)
        denominator = denominator + weight
        numerator = numerator + weight * parts_ref[source, :HEAD_SIZE, :].astype(jnp.float32)
    merged = (numerator * (1.0 / denominator)).astype(jnp.bfloat16)
    half_count = merged.shape[1] // PAIR
    for half in range(PAIR):
        for target in range(count):
            out_ref[half * count + target] = merged[:, half * half_count : (half + 1) * half_count]


def merge(parts):
    count, _, query_count = parts.shape
    return pl.pallas_call(
        merge_kernel,
        out_shape=jax.ShapeDtypeStruct(
            (PAIR * count, HEAD_SIZE, query_count // PAIR), jnp.bfloat16
        ),
        in_specs=[VMEM],
        out_specs=VMEM,
        compiler_params=pltpu.CompilerParams(vmem_limit_bytes=8 << 20),
        name="merge",
    )(parts)


def project_kernel(index_ref, heads_ref, own_ref, other_ref, out_ref):
    member = lax.rem(index_ref[2], PAIR)
    total = dot(heads_ref[member], own_ref[...], ((0,), (0,)))
    total += dot(heads_ref[1 - member], other_ref[...], ((0,), (0,)))
    out_ref[...] = total.astype(jnp.bfloat16)


def project(index, heads, own_weight, other_weight):
    return pl.pallas_call(
        project_kernel,
        out_shape=jax.ShapeDtypeStruct((heads.shape[2], own_weight.shape[1]), jnp.bfloat16),
        in_specs=[SMEM, VMEM, VMEM, VMEM],
        out_specs=VMEM,
        compiler_params=pltpu.CompilerParams(vmem_limit_bytes=16 << 20),
        name="project",
    )(index, heads, own_weight, other_weight)


def exchange(x, axis, groups=None):
    return lax.all_to_all(x, axis, 0, 0, tiled=True, axis_index_groups=groups)


def per_device(queries, keys, values, doc_ids, out_weight):
    key_index, tok_index, kv_index = (lax.axis_index(name) for name in ("key", "tok", "kv"))
    key_count, tok_count, kv_count = (lax.axis_size(name) for name in ("key", "tok", "kv"))
    row_count = queries.shape[0]
    slice_rows = row_count // tok_count
    index = jnp.stack([key_index, tok_index, kv_index])
    pair = jnp.concatenate(
        [
            lax.dynamic_slice_in_dim(keys, tok_index * slice_rows, slice_rows, 0),
            lax.dynamic_slice_in_dim(values, tok_index * slice_rows, slice_rows, 0),
        ],
        axis=1,
    )
    pairs = exchange(jnp.broadcast_to(pair[None], (key_count,) + pair.shape), "key")
    swap = [(member, member ^ 1) for member in range(kv_count)]
    other_weight = lax.ppermute(out_weight, "kv", swap)
    all_queries = lax.all_gather(queries, "tok", axis=0)
    first = find_first(index, doc_ids.reshape(-1, LANES), row_count, kv_count)
    parts = attend(index, first, all_queries, pairs, kv_count)
    parts = exchange(parts, "tok")
    merged = merge(parts)
    width = PAIR * tok_count
    groups = [
        [start + member for member in range(width)] for start in range(0, kv_count * tok_count, width)
    ]
    heads = exchange(merged, ("kv", "tok"), groups)
    heads = heads.reshape(PAIR, tok_count * HEAD_SIZE, row_count // PAIR)
    total = project(index, heads, out_weight, other_weight)
    total = total.reshape(kv_count, row_count // PAIR // kv_count, -1)
    shares = exchange(total, "kv")
    shares = shares.reshape((kv_count // PAIR, PAIR) + shares.shape[1:]).astype(jnp.float32)
    return jnp.sum(shares, axis=0).astype(jnp.bfloat16).reshape(row_count // kv_count, -1)


def solution(mesh):
    placed = (P("key", ("kv", "tok")), P("key", "kv"), P("key", "kv"), P(), P("kv", "tok"))

    return jax.shard_map(per_device, mesh=mesh, in_specs=placed, out_specs=P(("key", "kv"), "tok"), check_vma=False)
```

```python
import math

import jax
import jax.numpy as jnp
from jax import lax
from jax.experimental import pallas as pl
from jax.experimental.pallas import tpu as pltpu
from jax.sharding import PartitionSpec as P


HEAD_SIZE = 128
REACH = 8
LOW = -1e30
MOST_DOC = 5
LANES = 128
CORES = 2
PAIR = 2
NEEDED = REACH // PAIR
FACTOR = math.log2(math.e) / math.sqrt(HEAD_SIZE)

VMEM = pl.BlockSpec(memory_space=pltpu.VMEM)
SMEM = pl.BlockSpec(memory_space=pltpu.SMEM)


def dot(a, b, contract):
    return lax.dot_general(a, b, (contract, ((), ())), preferred_element_type=jnp.float32)


def first_kernel(index_ref, docs_ref, first_ref):
    query_count = first_ref.shape[1]
    docs = docs_ref[...]
    place = lax.broadcasted_iota(jnp.int32, (1, query_count), 1) + index_ref[0] * query_count
    place = place.astype(jnp.float32)
    first = jnp.zeros((1, query_count), jnp.float32)
    for number in range(1, MOST_DOC + 1):
        smaller = jnp.where(docs < number, 1.0, 0.0)
        begins = jnp.sum(jnp.sum(smaller, axis=0, keepdims=True), axis=1, keepdims=True)
        first = jnp.where(begins <= place, jnp.maximum(first, begins), first)
    first_ref[...] = first


def find_first(index, docs, query_count):
    return pl.pallas_call(
        first_kernel,
        out_shape=jax.ShapeDtypeStruct((1, query_count), jnp.float32),
        in_specs=[SMEM, VMEM],
        out_specs=VMEM,
        compiler_params=pltpu.CompilerParams(vmem_limit_bytes=4 << 20),
        name="first",
    )(index, docs)


def earliest(own, source_parity, taker_parity):
    return own // PAIR - NEEDED + taker_parity * (1 - source_parity)


def pick_kernel(index_ref, ranges_ref, out_ref):
    own = index_ref[0]
    count = ranges_ref.shape[0]
    takers = out_ref.shape[0] // PAIR
    for parity in range(PAIR):
        begin = earliest(own, lax.rem(own, PAIR), parity)
        for place in range(NEEDED):
            block = ranges_ref[lax.rem(begin + place + count, count)]
            for taker in range(takers):
                out_ref[parity * takers + taker, place] = block


def pick(index, ranges, taker_count):
    return pl.pallas_call(
        pick_kernel,
        out_shape=jax.ShapeDtypeStruct((taker_count, NEEDED) + ranges.shape[1:], jnp.bfloat16),
        in_specs=[SMEM, VMEM],
        out_specs=VMEM,
        compiler_params=pltpu.CompilerParams(vmem_limit_bytes=8 << 20),
        name="pick",
    )(index, ranges)


def mask_half(scores, own, core, first, blocks_shape, query_count):
    source_count, place_count, rows, _ = blocks_shape
    row = lax.broadcasted_iota(jnp.int32, (rows, query_count), 0).astype(jnp.float32)
    chips = source_count // PAIR
    pieces = []
    for source in range(source_count):
        parity, chip = source // chips, source % chips
        begin = earliest(own, parity, lax.rem(own, PAIR))
        for place in range(place_count):
            number = (begin + place) * PAIR + parity
            start = number * query_count + (chip * CORES + core) * rows
            at = (source * place_count + place) * rows
            allowed = row >= first - start.astype(jnp.float32)
            pieces.append(jnp.where(allowed, scores[at : at + rows] * FACTOR, LOW))
    return pieces


def near_kernel(
    index_ref, first_ref, queries_ref, keys_ref, values_ref, blocks_ref, stats_ref, sums_ref
):
    own, core = index_ref[0], lax.rem(index_ref[1], CORES)
    query_count = queries_ref.shape[0]
    first = first_ref[...]
    blocks = blocks_ref[...].reshape(-1, 2 * HEAD_SIZE)
    queries = queries_ref[...]
    scores = dot(blocks[:, :HEAD_SIZE], queries, ((1,), (1,)))
    pieces = mask_half(scores, own, core, first, blocks_ref.shape, query_count)
    scores = dot(keys_ref[...], queries, ((1,), (1,)))
    row = lax.broadcasted_iota(jnp.int32, scores.shape, 0)
    lane = lax.broadcasted_iota(jnp.int32, scores.shape, 1)
    begin = first - (own * query_count).astype(jnp.float32)
    allowed = (row <= lane) & (row.astype(jnp.float32) >= begin)
    pieces.append(jnp.where(allowed, scores * FACTOR, LOW))
    scores = jnp.concatenate(pieces, axis=0)
    highest = jnp.max(scores, axis=0, keepdims=True)
    weights = jnp.exp2(scores - highest)
    stats_ref[0:1, :] = highest
    stats_ref[1:2, :] = jnp.sum(weights, axis=0, keepdims=True)
    values = jnp.concatenate([blocks[:, HEAD_SIZE:], values_ref[...]], axis=0)
    sums_ref[...] = dot(values, weights.astype(jnp.bfloat16), ((0,), (0,)))


def far_kernel(index_ref, first_ref, queries_ref, blocks_ref, stats_ref, sums_ref, out_ref):
    own, core = index_ref[0], lax.rem(index_ref[1], CORES)
    query_count = queries_ref.shape[0]
    blocks = blocks_ref[...].reshape(-1, 2 * HEAD_SIZE)
    scores = dot(blocks[:, :HEAD_SIZE], queries_ref[...], ((1,), (1,)))
    pieces = mask_half(scores, own, 1 - core, first_ref[...], blocks_ref.shape, query_count)
    scores = jnp.concatenate(pieces, axis=0)
    before = stats_ref[0:1, :]
    highest = jnp.maximum(before, jnp.max(scores, axis=0, keepdims=True))
    weights = jnp.exp2(scores - highest)
    keep = jnp.exp2(before - highest)
    total = keep * stats_ref[1:2, :] + jnp.sum(weights, axis=0, keepdims=True)
    weighted = dot(blocks[:, HEAD_SIZE:], weights.astype(jnp.bfloat16), ((0,), (0,)))
    attn = ((keep * sums_ref[...] + weighted) * (1.0 / total)).astype(jnp.bfloat16)
    for target in range(out_ref.shape[0]):
        out_ref[target] = attn


def cost(queries, key_count):
    scores = queries.shape[0] * key_count
    return pl.CostEstimate(
        flops=4 * HEAD_SIZE * scores, transcendentals=scores, bytes_accessed=1 << 20
    )


def attend_near(index, first, queries, keys, values, blocks):
    query_count = queries.shape[0]
    return pl.pallas_call(
        near_kernel,
        out_shape=[
            jax.ShapeDtypeStruct((8, query_count), jnp.float32),
            jax.ShapeDtypeStruct((HEAD_SIZE, query_count), jnp.float32),
        ],
        in_specs=[SMEM] + [VMEM] * 5,
        out_specs=[VMEM, VMEM],
        compiler_params=pltpu.CompilerParams(vmem_limit_bytes=12 << 20),
        cost_estimate=cost(queries, 1280),
        name="near",
    )(index, first, queries, keys, values, blocks)


def attend_far(index, first, queries, blocks, stats, sums, target_count):
    query_count = queries.shape[0]
    return pl.pallas_call(
        far_kernel,
        out_shape=jax.ShapeDtypeStruct((target_count, HEAD_SIZE, query_count), jnp.bfloat16),
        in_specs=[SMEM] + [VMEM] * 5,
        out_specs=VMEM,
        compiler_params=pltpu.CompilerParams(vmem_limit_bytes=12 << 20),
        cost_estimate=cost(queries, 1024),
        name="far",
    )(index, first, queries, blocks, stats, sums)


def exchange(x, axis, groups=None):
    return lax.all_to_all(x, axis, 0, 0, tiled=True, axis_index_groups=groups)


def per_device(queries, keys, values, doc_ids, out_weight):
    key_index, tok_index = (lax.axis_index(name) for name in ("key", "tok"))
    key_count, tok_count, kv_count = (lax.axis_size(name) for name in ("key", "tok", "kv"))
    row_count = queries.shape[0]
    slice_rows = row_count // tok_count
    index = jnp.stack([key_index, tok_index])
    pair = jnp.concatenate(
        [
            lax.dynamic_slice_in_dim(keys, tok_index * slice_rows, slice_rows, 0),
            lax.dynamic_slice_in_dim(values, tok_index * slice_rows, slice_rows, 0),
        ],
        axis=1,
    )
    like = [[place * PAIR + parity for place in range(key_count // PAIR)] for parity in range(PAIR)]
    copies = jnp.broadcast_to(pair[None], (key_count // PAIR,) + pair.shape)
    ranges = exchange(copies, "key", like)
    first = find_first(index, doc_ids.reshape(-1, LANES), row_count)
    chips = tok_count // CORES
    beside = [
        [(begin + parity) * tok_count + chip * CORES + core for parity in range(PAIR) for chip in range(chips)]
        for begin in range(0, key_count, PAIR)
        for core in range(CORES)
    ]
    blocks = exchange(pick(index, ranges, PAIR * chips), ("key", "tok"), beside)
    other_blocks = lax.ppermute(blocks, "tok", [(i, i ^ 1) for i in range(tok_count)])
    stats, sums = attend_near(index, first, queries, keys, values, blocks)
    attn = attend_far(index, first, queries, other_blocks, stats, sums, tok_count)
    attn = exchange(attn, "tok").reshape(tok_count * HEAD_SIZE, row_count)
    total = jnp.einsum("kq,kn->qn", attn, out_weight, preferred_element_type=jnp.float32)
    total = total.astype(jnp.bfloat16).reshape(kv_count, row_count // kv_count, -1)
    shares = exchange(total, "kv")
    return jnp.sum(shares.astype(jnp.float32), axis=0).astype(jnp.bfloat16)


def solution(mesh):
    placed = (P("key", ("kv", "tok")), P("key", "kv"), P("key", "kv"), P(), P("kv", "tok"))

    return jax.shard_map(per_device, mesh=mesh, in_specs=placed, out_specs=P(("key", "kv"), "tok"), check_vma=False)
```

```python
import math

import jax
import jax.numpy as jnp
from jax import lax
from jax.experimental import pallas as pl
from jax.experimental.pallas import tpu as pltpu
from jax.sharding import PartitionSpec as P


HEAD_SIZE = 128
REACH = 8
LOW = -1e30
MOST_DOC = 5
LANES = 128
CORES = 2
PAIR = 2
NEEDED = REACH // PAIR
FACTOR = math.log2(math.e) / math.sqrt(HEAD_SIZE)

VMEM = pl.BlockSpec(memory_space=pltpu.VMEM)


def dot(a, b, contract):
    return lax.dot_general(a, b, (contract, ((), ())), preferred_element_type=jnp.float32)


def start_kernel(keys_ref, values_ref, docs_ref, out_ref, first_ref, pair_buf, docs_buf, sems):
    copy_count, rows, _ = out_ref.shape
    query_count = first_ref.shape[1]
    begin = pl.multiple_of(lax.axis_index("tok") * rows, rows)
    copies = [
        pltpu.make_async_copy(
            keys_ref.at[pl.ds(begin, rows), :], pair_buf.at[:, pl.ds(0, HEAD_SIZE)], sems.at[0]
        ),
        pltpu.make_async_copy(
            values_ref.at[pl.ds(begin, rows), :],
            pair_buf.at[:, pl.ds(HEAD_SIZE, HEAD_SIZE)],
            sems.at[1],
        ),
        pltpu.make_async_copy(docs_ref, docs_buf, sems.at[2]),
    ]
    for copy in copies:
        copy.start()
    for copy in copies:
        copy.wait()
    pair = pair_buf[...]
    for target in range(copy_count):
        out_ref[target] = pair
    docs = docs_buf[...]
    place = lax.broadcasted_iota(jnp.int32, (1, query_count), 1)
    place = (place + lax.axis_index("key") * query_count).astype(jnp.float32)
    first = jnp.zeros((1, query_count), jnp.float32)
    for number in range(1, MOST_DOC + 1):
        smaller = jnp.where(docs < number, 1.0, 0.0)
        begins = jnp.sum(jnp.sum(smaller, axis=0, keepdims=True), axis=1, keepdims=True)
        first = jnp.where(begins <= place, jnp.maximum(first, begins), first)
    first_ref[...] = first


def start(keys, values, docs, copy_count, rows):
    query_count = keys.shape[0]
    hbm = pl.BlockSpec(memory_space=pltpu.HBM)
    return pl.pallas_call(
        start_kernel,
        out_shape=[
            jax.ShapeDtypeStruct((copy_count, rows, 2 * HEAD_SIZE), jnp.bfloat16),
            jax.ShapeDtypeStruct((1, query_count), jnp.float32),
        ],
        in_specs=[hbm, hbm, hbm],
        out_specs=[VMEM, VMEM],
        scratch_shapes=[
            pltpu.VMEM((rows, 2 * HEAD_SIZE), jnp.bfloat16),
            pltpu.VMEM(docs.shape, jnp.int32),
            pltpu.SemaphoreType.DMA((3,)),
        ],
        compiler_params=pltpu.CompilerParams(vmem_limit_bytes=4 << 20),
        name="start",
    )(*(pltpu.with_memory_space_constraint(x, pltpu.HBM) for x in (keys, values, docs)))


def earliest(own, source_parity, taker_parity):
    return own // PAIR - NEEDED + taker_parity * (1 - source_parity)


def pick_kernel(ranges_ref, out_ref):
    own = lax.axis_index("key")
    count = ranges_ref.shape[0]
    takers = out_ref.shape[0] // PAIR
    for parity in range(PAIR):
        begin = earliest(own, lax.rem(own, PAIR), parity)
        for place in range(NEEDED):
            block = ranges_ref[lax.rem(begin + place + count, count)]
            for taker in range(takers):
                out_ref[parity * takers + taker, place] = block


def pick(ranges, taker_count):
    return pl.pallas_call(
        pick_kernel,
        out_shape=jax.ShapeDtypeStruct((taker_count, NEEDED) + ranges.shape[1:], jnp.bfloat16),
        in_specs=[VMEM],
        out_specs=VMEM,
        compiler_params=pltpu.CompilerParams(vmem_limit_bytes=8 << 20),
        name="pick",
    )(ranges)


def mask_half(scores, own, core, first, blocks_shape, query_count):
    source_count, place_count, rows, _ = blocks_shape
    row = lax.broadcasted_iota(jnp.int32, (rows, query_count), 0).astype(jnp.float32)
    chips = source_count // PAIR
    pieces = []
    for source in range(source_count):
        parity, chip = source // chips, source % chips
        begin = earliest(own, parity, lax.rem(own, PAIR))
        for place in range(place_count):
            number = (begin + place) * PAIR + parity
            start = number * query_count + (chip * CORES + core) * rows
            at = (source * place_count + place) * rows
            allowed = row >= first - start.astype(jnp.float32)
            pieces.append(jnp.where(allowed, scores[at : at + rows] * FACTOR, LOW))
    return pieces


def near_kernel(
    first_ref, queries_ref, keys_ref, values_ref, blocks_ref, stats_ref, sums_ref
):
    own, core = lax.axis_index("key"), lax.rem(lax.axis_index("tok"), CORES)
    query_count = queries_ref.shape[0]
    first = first_ref[...]
    blocks = blocks_ref[...].reshape(-1, 2 * HEAD_SIZE)
    queries = queries_ref[...]
    scores = dot(blocks[:, :HEAD_SIZE], queries, ((1,), (1,)))
    pieces = mask_half(scores, own, core, first, blocks_ref.shape, query_count)
    scores = dot(keys_ref[...], queries, ((1,), (1,)))
    row = lax.broadcasted_iota(jnp.int32, scores.shape, 0)
    lane = lax.broadcasted_iota(jnp.int32, scores.shape, 1)
    begin = first - (own * query_count).astype(jnp.float32)
    allowed = (row <= lane) & (row.astype(jnp.float32) >= begin)
    pieces.append(jnp.where(allowed, scores * FACTOR, LOW))
    scores = jnp.concatenate(pieces, axis=0)
    highest = jnp.max(scores, axis=0, keepdims=True)
    weights = jnp.exp2(scores - highest)
    stats_ref[0:1, :] = highest
    stats_ref[1:2, :] = jnp.sum(weights, axis=0, keepdims=True)
    values = jnp.concatenate([blocks[:, HEAD_SIZE:], values_ref[...]], axis=0)
    sums_ref[...] = dot(values, weights.astype(jnp.bfloat16), ((0,), (0,)))


def far_kernel(first_ref, queries_ref, blocks_ref, stats_ref, sums_ref, out_ref):
    own, core = lax.axis_index("key"), lax.rem(lax.axis_index("tok"), CORES)
    query_count = queries_ref.shape[0]
    blocks = blocks_ref[...].reshape(-1, 2 * HEAD_SIZE)
    scores = dot(blocks[:, :HEAD_SIZE], queries_ref[...], ((1,), (1,)))
    pieces = mask_half(scores, own, 1 - core, first_ref[...], blocks_ref.shape, query_count)
    scores = jnp.concatenate(pieces, axis=0)
    before = stats_ref[0:1, :]
    highest = jnp.maximum(before, jnp.max(scores, axis=0, keepdims=True))
    weights = jnp.exp2(scores - highest)
    keep = jnp.exp2(before - highest)
    total = keep * stats_ref[1:2, :] + jnp.sum(weights, axis=0, keepdims=True)
    weighted = dot(blocks[:, HEAD_SIZE:], weights.astype(jnp.bfloat16), ((0,), (0,)))
    attn = ((keep * sums_ref[...] + weighted) * (1.0 / total)).astype(jnp.bfloat16)
    for target in range(out_ref.shape[0]):
        out_ref[target] = attn


def cost(queries, key_count):
    scores = queries.shape[0] * key_count
    return pl.CostEstimate(
        flops=4 * HEAD_SIZE * scores, transcendentals=scores, bytes_accessed=1 << 20
    )


def attend_near(first, queries, keys, values, blocks):
    query_count = queries.shape[0]
    return pl.pallas_call(
        near_kernel,
        out_shape=[
            jax.ShapeDtypeStruct((8, query_count), jnp.float32),
            jax.ShapeDtypeStruct((HEAD_SIZE, query_count), jnp.float32),
        ],
        in_specs=[VMEM] * 5,
        out_specs=[VMEM, VMEM],
        compiler_params=pltpu.CompilerParams(vmem_limit_bytes=12 << 20),
        cost_estimate=cost(queries, 1280),
        name="near",
    )(first, queries, keys, values, blocks)


def attend_far(first, queries, blocks, stats, sums, target_count):
    query_count = queries.shape[0]
    return pl.pallas_call(
        far_kernel,
        out_shape=jax.ShapeDtypeStruct((target_count, HEAD_SIZE, query_count), jnp.bfloat16),
        in_specs=[VMEM] * 5,
        out_specs=VMEM,
        compiler_params=pltpu.CompilerParams(vmem_limit_bytes=12 << 20),
        cost_estimate=cost(queries, 1024),
        name="far",
    )(first, queries, blocks, stats, sums)


def exchange(x, axis, groups=None):
    return lax.all_to_all(x, axis, 0, 0, tiled=True, axis_index_groups=groups)


def per_device(queries, keys, values, doc_ids, out_weight):
    key_count, tok_count, kv_count = (lax.axis_size(name) for name in ("key", "tok", "kv"))
    row_count = queries.shape[0]
    like = [[place * PAIR + parity for place in range(key_count // PAIR)] for parity in range(PAIR)]
    copies, first = start(
        keys, values, doc_ids.reshape(-1, LANES), key_count // PAIR, row_count // tok_count
    )
    ranges = exchange(copies, "key", like)
    chips = tok_count // CORES
    beside = [
        [(begin + parity) * tok_count + chip * CORES + core for parity in range(PAIR) for chip in range(chips)]
        for begin in range(0, key_count, PAIR)
        for core in range(CORES)
    ]
    blocks = exchange(pick(ranges, PAIR * chips), ("key", "tok"), beside)
    other_blocks = lax.ppermute(blocks, "tok", [(i, i ^ 1) for i in range(tok_count)])
    stats, sums = attend_near(first, queries, keys, values, blocks)
    attn = attend_far(first, queries, other_blocks, stats, sums, tok_count)
    attn = exchange(attn, "tok").reshape(tok_count * HEAD_SIZE, row_count)
    total = jnp.einsum("kq,kn->qn", attn, out_weight, preferred_element_type=jnp.float32)
    total = total.astype(jnp.bfloat16).reshape(kv_count, row_count // kv_count, -1)
    shares = exchange(total, "kv")
    return jnp.sum(shares.astype(jnp.float32), axis=0).astype(jnp.bfloat16)


def solution(mesh):
    placed = (P("key", ("kv", "tok")), P("key", "kv"), P("key", "kv"), P(), P("kv", "tok"))

    return jax.shard_map(per_device, mesh=mesh, in_specs=placed, out_specs=P(("key", "kv"), "tok"), check_vma=False)
```

```python
import math

import jax
import jax.numpy as jnp
from jax import lax
from jax.experimental import pallas as pl
from jax.experimental.pallas import tpu as pltpu
from jax.sharding import PartitionSpec as P


HEAD_SIZE = 128
REACH = 8
LOW = -1e30
MOST_DOC = 5
LANES = 128
CORES = 2
PAIR = 2
FACTOR = math.log2(math.e) / math.sqrt(HEAD_SIZE)

VMEM = pl.BlockSpec(memory_space=pltpu.VMEM)


def dot(a, b, contract):
    return lax.dot_general(a, b, (contract, ((), ())), preferred_element_type=jnp.float32)


def start_kernel(
    queries_ref, keys_ref, values_ref, docs_ref, out_ref, first_ref, own_ref, docs_buf, sems
):
    rows = out_ref.shape[0]
    query_count = first_ref.shape[1]
    begin = pl.multiple_of(lax.rem(lax.axis_index("tok"), CORES) * rows, rows)
    copies = [pltpu.make_async_copy(docs_ref, docs_buf, sems.at[0])]
    for place, source in enumerate((keys_ref, values_ref, queries_ref)):
        copies.append(pltpu.make_async_copy(source, own_ref.at[place], sems.at[place + 1]))
    for copy in copies:
        copy.start()
    for copy in copies:
        copy.wait()
    out_ref[:, :HEAD_SIZE] = own_ref[0, pl.ds(begin, rows), :]
    out_ref[:, HEAD_SIZE:] = own_ref[1, pl.ds(begin, rows), :]
    docs = docs_buf[...]
    place = lax.broadcasted_iota(jnp.int32, (1, query_count), 1)
    place = (place + lax.axis_index("key") * query_count).astype(jnp.float32)
    first = jnp.zeros((1, query_count), jnp.float32)
    for number in range(1, MOST_DOC + 1):
        smaller = jnp.where(docs < number, 1.0, 0.0)
        begins = jnp.sum(jnp.sum(smaller, axis=0, keepdims=True), axis=1, keepdims=True)
        first = jnp.where(begins <= place, jnp.maximum(first, begins), first)
    first_ref[...] = first


def start(queries, keys, values, docs):
    query_count = keys.shape[0]
    hbm = pl.BlockSpec(memory_space=pltpu.HBM)
    return pl.pallas_call(
        start_kernel,
        out_shape=[
            jax.ShapeDtypeStruct((query_count // CORES, 2 * HEAD_SIZE), jnp.bfloat16),
            jax.ShapeDtypeStruct((1, query_count), jnp.float32),
            jax.ShapeDtypeStruct((3,) + keys.shape, jnp.bfloat16),
        ],
        in_specs=[hbm] * 4,
        out_specs=[VMEM] * 3,
        scratch_shapes=[
            pltpu.VMEM(docs.shape, jnp.int32),
            pltpu.SemaphoreType.DMA((4,)),
        ],
        compiler_params=pltpu.CompilerParams(vmem_limit_bytes=4 << 20),
        name="start",
    )(*(pltpu.with_memory_space_constraint(x, pltpu.HBM) for x in (queries, keys, values, docs)))


def shift_of(chip, core):
    return jnp.where(core == 0, REACH - PAIR * chip, PAIR + PAIR * chip)


def pick_kernel(half_ref, held_ref, out_ref):
    own, tok = lax.axis_index("key"), lax.axis_index("tok")
    takers = out_ref.shape[0] // PAIR
    held = held_ref[...]
    swapped = (lax.rem(own, PAIR) == 0) & (shift_of(tok // CORES, lax.rem(tok, CORES)) == REACH)
    for taker in range(takers):
        out_ref[taker] = held
    beside = jnp.where(swapped, half_ref[...].astype(jnp.float32), held.astype(jnp.float32))
    beside = beside.astype(jnp.bfloat16)
    for taker in range(takers):
        out_ref[takers + taker] = beside


def pick(half, held, taker_count):
    return pl.pallas_call(
        pick_kernel,
        out_shape=jax.ShapeDtypeStruct((taker_count,) + held.shape, jnp.bfloat16),
        in_specs=[VMEM, VMEM],
        out_specs=VMEM,
        compiler_params=pltpu.CompilerParams(vmem_limit_bytes=8 << 20),
        name="pick",
    )(half, held)


def mask_half(scores, own, core, first, blocks_shape, query_count):
    source_count, rows, _ = blocks_shape
    row = lax.broadcasted_iota(jnp.int32, (rows, query_count), 0).astype(jnp.float32)
    chips = source_count // PAIR
    pieces = []
    for source in range(source_count):
        parity, chip = source // chips, source % chips
        shift = shift_of(chip, core)
        if parity == 0:
            shift = jnp.where((lax.rem(own, PAIR) == 1) & (shift == REACH), 0, shift)
        number = own // PAIR * PAIR + parity - shift
        start = number * query_count + core * rows
        allowed = row >= first - start.astype(jnp.float32)
        pieces.append(jnp.where(allowed, scores[source * rows : (source + 1) * rows] * FACTOR, LOW))
    return pieces


def near_kernel(first_ref, own_ref, blocks_ref, stats_ref, sums_ref):
    own, core = lax.axis_index("key"), lax.rem(lax.axis_index("tok"), CORES)
    query_count = first_ref.shape[1]
    first = first_ref[...]
    blocks = blocks_ref[...].reshape(-1, 2 * HEAD_SIZE)
    queries = own_ref[2]
    scores = dot(blocks[:, :HEAD_SIZE], queries, ((1,), (1,)))
    pieces = mask_half(scores, own, core, first, blocks_ref.shape, query_count)
    scores = dot(own_ref[0], queries, ((1,), (1,)))
    row = lax.broadcasted_iota(jnp.int32, scores.shape, 0)
    lane = lax.broadcasted_iota(jnp.int32, scores.shape, 1)
    begin = first - (own * query_count).astype(jnp.float32)
    allowed = (row <= lane) & (row.astype(jnp.float32) >= begin)
    pieces.append(jnp.where(allowed, scores * FACTOR, LOW))
    scores = jnp.concatenate(pieces, axis=0)
    highest = jnp.max(scores, axis=0, keepdims=True)
    weights = jnp.exp2(scores - highest)
    stats_ref[0:1, :] = highest
    stats_ref[1:2, :] = jnp.sum(weights, axis=0, keepdims=True)
    values = jnp.concatenate([blocks[:, HEAD_SIZE:], own_ref[1]], axis=0)
    sums_ref[...] = dot(values, weights.astype(jnp.bfloat16), ((0,), (0,)))


def far_kernel(first_ref, own_ref, blocks_ref, stats_ref, sums_ref, out_ref):
    own, core = lax.axis_index("key"), lax.rem(lax.axis_index("tok"), CORES)
    query_count = first_ref.shape[1]
    blocks = blocks_ref[...].reshape(-1, 2 * HEAD_SIZE)
    scores = dot(blocks[:, :HEAD_SIZE], own_ref[2], ((1,), (1,)))
    pieces = mask_half(scores, own, 1 - core, first_ref[...], blocks_ref.shape, query_count)
    scores = jnp.concatenate(pieces, axis=0)
    before = stats_ref[0:1, :]
    highest = jnp.maximum(before, jnp.max(scores, axis=0, keepdims=True))
    weights = jnp.exp2(scores - highest)
    keep = jnp.exp2(before - highest)
    total = keep * stats_ref[1:2, :] + jnp.sum(weights, axis=0, keepdims=True)
    weighted = dot(blocks[:, HEAD_SIZE:], weights.astype(jnp.bfloat16), ((0,), (0,)))
    attn = ((keep * sums_ref[...] + weighted) * (1.0 / total)).astype(jnp.bfloat16)
    for target in range(out_ref.shape[0]):
        out_ref[target] = attn


def cost(query_count, key_count):
    scores = query_count * key_count
    return pl.CostEstimate(
        flops=4 * HEAD_SIZE * scores, transcendentals=scores, bytes_accessed=1 << 20
    )


def attend_near(first, own, blocks):
    query_count = first.shape[1]
    return pl.pallas_call(
        near_kernel,
        out_shape=[
            jax.ShapeDtypeStruct((8, query_count), jnp.float32),
            jax.ShapeDtypeStruct((HEAD_SIZE, query_count), jnp.float32),
        ],
        in_specs=[VMEM] * 3,
        out_specs=[VMEM, VMEM],
        compiler_params=pltpu.CompilerParams(vmem_limit_bytes=12 << 20),
        cost_estimate=cost(query_count, blocks.shape[0] * blocks.shape[1] + query_count),
        name="near",
    )(first, own, blocks)


def attend_far(first, own, blocks, stats, sums, target_count):
    query_count = first.shape[1]
    return pl.pallas_call(
        far_kernel,
        out_shape=jax.ShapeDtypeStruct((target_count, HEAD_SIZE, query_count), jnp.bfloat16),
        in_specs=[VMEM] * 5,
        out_specs=VMEM,
        compiler_params=pltpu.CompilerParams(vmem_limit_bytes=12 << 20),
        cost_estimate=cost(query_count, blocks.shape[0] * blocks.shape[1]),
        name="far",
    )(first, own, blocks, stats, sums)


def exchange(x, axis, groups=None):
    return lax.all_to_all(x, axis, 0, 0, tiled=True, axis_index_groups=groups)


def per_device(queries, keys, values, doc_ids, out_weight):
    key_count, tok_count, kv_count = (lax.axis_size(name) for name in ("key", "tok", "kv"))
    row_count = queries.shape[0]
    half, first, own = start(queries, keys, values, doc_ids.reshape(-1, LANES))
    chips = tok_count // CORES
    beside = [
        [(begin + parity) * tok_count + chip * CORES + core for parity in range(PAIR) for chip in range(chips)]
        for begin in range(0, key_count, PAIR)
        for core in range(CORES)
    ]
    shifts = [REACH - tok if tok % CORES == 0 else PAIR + tok - 1 for tok in range(tok_count)]
    later = [
        (begin * tok_count + tok, (begin + shifts[tok]) * tok_count + tok)
        for begin in range(key_count)
        for tok in range(tok_count)
        if begin + shifts[tok] < key_count
    ]
    held = lax.ppermute(half, ("key", "tok"), later)
    blocks = exchange(pick(half, held, PAIR * chips), ("key", "tok"), beside)
    other_blocks = lax.ppermute(blocks, "tok", [(i, i ^ 1) for i in range(tok_count)])
    stats, sums = attend_near(first, own, blocks)
    attn = attend_far(first, own, other_blocks, stats, sums, tok_count)
    attn = exchange(attn, "tok").reshape(tok_count * HEAD_SIZE, row_count)
    total = jnp.einsum("kq,kn->qn", attn, out_weight, preferred_element_type=jnp.float32)
    total = total.astype(jnp.bfloat16).reshape(kv_count, row_count // kv_count, -1)
    shares = exchange(total, "kv")
    return jnp.sum(shares.astype(jnp.float32), axis=0).astype(jnp.bfloat16)


def solution(mesh):
    placed = (P("key", ("kv", "tok")), P("key", "kv"), P("key", "kv"), P(), P("kv", "tok"))

    return jax.shard_map(per_device, mesh=mesh, in_specs=placed, out_specs=P(("key", "kv"), "tok"), check_vma=False)
```

```python
import math

import jax
import jax.numpy as jnp
from jax import lax
from jax.experimental import pallas as pl
from jax.experimental.pallas import tpu as pltpu
from jax.sharding import PartitionSpec as P


HEAD_SIZE = 128
REACH = 8
LOW = -1e30
MOST_DOC = 5
LANES = 128
CORES = 2
PAIR = 2
FACTOR = math.log2(math.e) / math.sqrt(HEAD_SIZE)

VMEM = pl.BlockSpec(memory_space=pltpu.VMEM)


def dot(a, b, contract):
    return lax.dot_general(a, b, (contract, ((), ())), preferred_element_type=jnp.float32)


def start_kernel(keys_ref, values_ref, out_ref, sems):
    rows = out_ref.shape[0]
    tok = lax.axis_index("tok")
    shift = shift_of(tok // CORES, lax.rem(tok, CORES))
    begin = pl.multiple_of(lax.rem(tok, CORES) * rows, rows)

    @pl.when(lax.axis_index("key") + shift < lax.axis_size("key"))
    def _():
        copies = [
            pltpu.make_async_copy(
                source.at[pl.ds(begin, rows), :],
                out_ref.at[:, pl.ds(place * HEAD_SIZE, HEAD_SIZE)],
                sems.at[place],
            )
            for place, source in enumerate((keys_ref, values_ref))
        ]
        for copy in copies:
            copy.start()
        for copy in copies:
            copy.wait()


def start(keys, values):
    hbm = pl.BlockSpec(memory_space=pltpu.HBM)
    return pl.pallas_call(
        start_kernel,
        out_shape=jax.ShapeDtypeStruct((keys.shape[0] // CORES, 2 * HEAD_SIZE), jnp.bfloat16),
        in_specs=[hbm] * 2,
        out_specs=VMEM,
        scratch_shapes=[pltpu.SemaphoreType.DMA((2,))],
        compiler_params=pltpu.CompilerParams(vmem_limit_bytes=4 << 20),
        name="start",
    )(*(pltpu.with_memory_space_constraint(x, pltpu.HBM) for x in (keys, values)))


def load_kernel(queries_ref, keys_ref, values_ref, docs_ref, own_ref, docs_out_ref, sems):
    copies = [
        pltpu.make_async_copy(source, own_ref.at[place], sems.at[place])
        for place, source in enumerate((keys_ref, values_ref, queries_ref))
    ]
    copies.append(pltpu.make_async_copy(docs_ref, docs_out_ref, sems.at[3]))
    for copy in copies:
        copy.start()
    for copy in copies:
        copy.wait()


def load(*arrays):
    _, keys, _, docs = arrays
    hbm = pl.BlockSpec(memory_space=pltpu.HBM)
    return pl.pallas_call(
        load_kernel,
        out_shape=[
            jax.ShapeDtypeStruct((3,) + keys.shape, jnp.bfloat16),
            jax.ShapeDtypeStruct(docs.shape, jnp.int32),
        ],
        in_specs=[hbm] * 4,
        out_specs=[VMEM] * 2,
        scratch_shapes=[pltpu.SemaphoreType.DMA((4,))],
        compiler_params=pltpu.CompilerParams(vmem_limit_bytes=4 << 20),
        name="load",
    )(*(pltpu.with_memory_space_constraint(x, pltpu.HBM) for x in arrays))


def find_first(docs_ref, own, query_count):
    docs = docs_ref[...]
    place = lax.broadcasted_iota(jnp.int32, (1, query_count), 1)
    place = (place + own * query_count).astype(jnp.float32)
    first = jnp.zeros((1, query_count), jnp.float32)
    for number in range(1, MOST_DOC + 1):
        smaller = jnp.where(docs < number, 1.0, 0.0)
        begins = jnp.sum(jnp.sum(smaller, axis=0, keepdims=True), axis=1, keepdims=True)
        first = jnp.where(begins <= place, jnp.maximum(first, begins), first)
    return first


def shift_of(chip, core):
    return jnp.where(core == 0, REACH - PAIR * chip, PAIR + PAIR * chip)


def pick_kernel(own_ref, held_ref, out_ref):
    own, tok = lax.axis_index("key"), lax.axis_index("tok")
    rows = held_ref.shape[0]
    takers = out_ref.shape[0] // PAIR
    swapped = (lax.rem(own, PAIR) == 0) & (shift_of(tok // CORES, lax.rem(tok, CORES)) == REACH)
    held = held_ref[...]
    for taker in range(takers):
        out_ref[taker] = held

    @pl.when(swapped)
    def _():
        begin = pl.multiple_of(lax.rem(tok, CORES) * rows, rows)
        half = pl.ds(begin, rows)
        pair = jnp.concatenate([own_ref[0, half, :], own_ref[1, half, :]], axis=1)
        for taker in range(takers):
            out_ref[takers + taker] = pair

    @pl.when(jnp.logical_not(swapped))
    def _():
        for taker in range(takers):
            out_ref[takers + taker] = held_ref[...]


def pick(own, held, taker_count):
    return pl.pallas_call(
        pick_kernel,
        out_shape=jax.ShapeDtypeStruct((taker_count,) + held.shape, jnp.bfloat16),
        in_specs=[VMEM, VMEM],
        out_specs=VMEM,
        compiler_params=pltpu.CompilerParams(vmem_limit_bytes=8 << 20),
        name="pick",
    )(own, held)


def mask_half(scores, own, core, first, blocks_shape, query_count):
    source_count, rows, _ = blocks_shape
    row = lax.broadcasted_iota(jnp.int32, (rows, query_count), 0).astype(jnp.float32)
    chips = source_count // PAIR
    pieces = []
    for source in range(source_count):
        parity, chip = source // chips, source % chips
        shift = shift_of(chip, core)
        if parity == 0:
            shift = jnp.where((lax.rem(own, PAIR) == 1) & (shift == REACH), 0, shift)
        number = own // PAIR * PAIR + parity - shift
        start = number * query_count + core * rows
        allowed = row >= first - start.astype(jnp.float32)
        pieces.append(jnp.where(allowed, scores[source * rows : (source + 1) * rows] * FACTOR, LOW))
    return pieces


def near_kernel(docs_ref, own_ref, blocks_ref, first_ref, stats_ref, sums_ref):
    own, core = lax.axis_index("key"), lax.rem(lax.axis_index("tok"), CORES)
    query_count = first_ref.shape[1]
    first = find_first(docs_ref, own, query_count)
    first_ref[...] = first
    blocks = blocks_ref[...].reshape(-1, 2 * HEAD_SIZE)
    queries = own_ref[2]
    scores = dot(blocks[:, :HEAD_SIZE], queries, ((1,), (1,)))
    pieces = mask_half(scores, own, core, first, blocks_ref.shape, query_count)
    scores = dot(own_ref[0], queries, ((1,), (1,)))
    row = lax.broadcasted_iota(jnp.int32, scores.shape, 0)
    lane = lax.broadcasted_iota(jnp.int32, scores.shape, 1)
    begin = first - (own * query_count).astype(jnp.float32)
    allowed = (row <= lane) & (row.astype(jnp.float32) >= begin)
    pieces.append(jnp.where(allowed, scores * FACTOR, LOW))
    scores = jnp.concatenate(pieces, axis=0)
    highest = jnp.max(scores, axis=0, keepdims=True)
    weights = jnp.exp2(scores - highest)
    stats_ref[0:1, :] = highest
    stats_ref[1:2, :] = jnp.sum(weights, axis=0, keepdims=True)
    values = jnp.concatenate([blocks[:, HEAD_SIZE:], own_ref[1]], axis=0)
    sums_ref[...] = dot(values, weights.astype(jnp.bfloat16), ((0,), (0,)))


def far_kernel(first_ref, own_ref, blocks_ref, stats_ref, sums_ref, out_ref):
    own, core = lax.axis_index("key"), lax.rem(lax.axis_index("tok"), CORES)
    query_count = first_ref.shape[1]
    blocks = blocks_ref[...].reshape(-1, 2 * HEAD_SIZE)
    scores = dot(blocks[:, :HEAD_SIZE], own_ref[2], ((1,), (1,)))
    pieces = mask_half(scores, own, 1 - core, first_ref[...], blocks_ref.shape, query_count)
    scores = jnp.concatenate(pieces, axis=0)
    before = stats_ref[0:1, :]
    highest = jnp.maximum(before, jnp.max(scores, axis=0, keepdims=True))
    weights = jnp.exp2(scores - highest)
    keep = jnp.exp2(before - highest)
    total = keep * stats_ref[1:2, :] + jnp.sum(weights, axis=0, keepdims=True)
    weighted = dot(blocks[:, HEAD_SIZE:], weights.astype(jnp.bfloat16), ((0,), (0,)))
    attn = ((keep * sums_ref[...] + weighted) * (1.0 / total)).astype(jnp.bfloat16)
    for target in range(out_ref.shape[0]):
        out_ref[target] = attn


def cost(query_count, key_count):
    scores = query_count * key_count
    return pl.CostEstimate(
        flops=4 * HEAD_SIZE * scores, transcendentals=scores, bytes_accessed=1 << 20
    )


def attend_near(docs, own, blocks):
    query_count = own.shape[1]
    return pl.pallas_call(
        near_kernel,
        out_shape=[
            jax.ShapeDtypeStruct((1, query_count), jnp.float32),
            jax.ShapeDtypeStruct((8, query_count), jnp.float32),
            jax.ShapeDtypeStruct((HEAD_SIZE, query_count), jnp.float32),
        ],
        in_specs=[VMEM] * 3,
        out_specs=[VMEM] * 3,
        compiler_params=pltpu.CompilerParams(vmem_limit_bytes=12 << 20),
        cost_estimate=cost(query_count, blocks.shape[0] * blocks.shape[1] + query_count),
        name="near",
    )(docs, own, blocks)


def attend_far(first, own, blocks, stats, sums, target_count):
    query_count = first.shape[1]
    return pl.pallas_call(
        far_kernel,
        out_shape=jax.ShapeDtypeStruct((target_count, HEAD_SIZE, query_count), jnp.bfloat16),
        in_specs=[VMEM] * 5,
        out_specs=VMEM,
        compiler_params=pltpu.CompilerParams(vmem_limit_bytes=12 << 20),
        cost_estimate=cost(query_count, blocks.shape[0] * blocks.shape[1]),
        name="far",
    )(first, own, blocks, stats, sums)


def exchange(x, axis, groups=None):
    return lax.all_to_all(x, axis, 0, 0, tiled=True, axis_index_groups=groups)


def per_device(queries, keys, values, doc_ids, out_weight):
    key_count, tok_count, kv_count = (lax.axis_size(name) for name in ("key", "tok", "kv"))
    row_count = queries.shape[0]
    chips = tok_count // CORES
    beside = [
        [(begin + parity) * tok_count + chip * CORES + core for parity in range(PAIR) for chip in range(chips)]
        for begin in range(0, key_count, PAIR)
        for core in range(CORES)
    ]
    shifts = [REACH - tok if tok % CORES == 0 else PAIR + tok - 1 for tok in range(tok_count)]
    later = [
        (begin * tok_count + tok, (begin + shifts[tok]) * tok_count + tok)
        for begin in range(key_count)
        for tok in range(tok_count)
        if begin + shifts[tok] < key_count
    ]
    half = start(keys, values)
    held = lax.ppermute(half, ("key", "tok"), later)
    own, docs = load(queries, keys, values, doc_ids.reshape(-1, LANES))
    blocks = exchange(pick(own, held, PAIR * chips), ("key", "tok"), beside)
    other_blocks = lax.ppermute(blocks, "tok", [(i, i ^ 1) for i in range(tok_count)])
    first, stats, sums = attend_near(docs, own, blocks)
    attn = attend_far(first, own, other_blocks, stats, sums, tok_count)
    attn = exchange(attn, "tok").reshape(tok_count * HEAD_SIZE, row_count)
    total = jnp.einsum("kq,kn->qn", attn, out_weight, preferred_element_type=jnp.float32)
    total = total.astype(jnp.bfloat16).reshape(kv_count, row_count // kv_count, -1)
    shares = exchange(total, "kv")
    return jnp.sum(shares.astype(jnp.float32), axis=0).astype(jnp.bfloat16)


def solution(mesh):
    placed = (P("key", ("kv", "tok")), P("key", "kv"), P("key", "kv"), P(), P("kv", "tok"))

    return jax.shard_map(
        per_device, mesh=mesh, in_specs=placed, out_specs=P(("key", "kv"), "tok"), check_vma=False
    )
```

```python
import math

import jax
import jax.numpy as jnp
from jax import lax
from jax.experimental import pallas as pl
from jax.experimental.pallas import tpu as pltpu
from jax.sharding import PartitionSpec as P


HEAD_SIZE = 128
REACH = 8
LOW = -1e30
MOST_DOC = 5
LANES = 128
CORES = 2
PAIR = 2
FACTOR = math.log2(math.e) / math.sqrt(HEAD_SIZE)

VMEM = pl.BlockSpec(memory_space=pltpu.VMEM)


def dot(a, b, contract):
    return lax.dot_general(a, b, (contract, ((), ())), preferred_element_type=jnp.float32)


def start_kernel(keys_ref, values_ref, out_ref, sems):
    rows = out_ref.shape[0]
    tok = lax.axis_index("tok")
    shift = shift_of(tok // CORES, lax.rem(tok, CORES))
    begin = pl.multiple_of(lax.rem(tok, CORES) * rows, rows)

    @pl.when(lax.axis_index("key") + shift < lax.axis_size("key"))
    def _():
        copies = [
            pltpu.make_async_copy(
                source.at[pl.ds(begin, rows), :],
                out_ref.at[:, pl.ds(place * HEAD_SIZE, HEAD_SIZE)],
                sems.at[place],
            )
            for place, source in enumerate((keys_ref, values_ref))
        ]
        for copy in copies:
            copy.start()
        for copy in copies:
            copy.wait()


def start(keys, values):
    hbm = pl.BlockSpec(memory_space=pltpu.HBM)
    return pl.pallas_call(
        start_kernel,
        out_shape=jax.ShapeDtypeStruct((keys.shape[0] // CORES, 2 * HEAD_SIZE), jnp.bfloat16),
        in_specs=[hbm] * 2,
        out_specs=VMEM,
        scratch_shapes=[pltpu.SemaphoreType.DMA((2,))],
        compiler_params=pltpu.CompilerParams(vmem_limit_bytes=4 << 20),
        name="start",
    )(*(pltpu.with_memory_space_constraint(x, pltpu.HBM) for x in (keys, values)))


def load_kernel(queries_ref, keys_ref, values_ref, docs_ref, own_ref, docs_out_ref, sems):
    copies = [
        pltpu.make_async_copy(source, own_ref.at[place], sems.at[place])
        for place, source in enumerate((keys_ref, values_ref, queries_ref))
    ]
    copies.append(pltpu.make_async_copy(docs_ref, docs_out_ref, sems.at[3]))
    for copy in copies:
        copy.start()
    for copy in copies:
        copy.wait()


def load(*arrays):
    _, keys, _, docs = arrays
    hbm = pl.BlockSpec(memory_space=pltpu.HBM)
    return pl.pallas_call(
        load_kernel,
        out_shape=[
            jax.ShapeDtypeStruct((3,) + keys.shape, jnp.bfloat16),
            jax.ShapeDtypeStruct(docs.shape, jnp.int32),
        ],
        in_specs=[hbm] * 4,
        out_specs=[VMEM] * 2,
        scratch_shapes=[pltpu.SemaphoreType.DMA((4,))],
        compiler_params=pltpu.CompilerParams(vmem_limit_bytes=4 << 20),
        name="load",
    )(*(pltpu.with_memory_space_constraint(x, pltpu.HBM) for x in arrays))


def find_first(docs_ref, own, query_count):
    docs = docs_ref[...]
    place = lax.broadcasted_iota(jnp.int32, (1, query_count), 1)
    place = (place + own * query_count).astype(jnp.float32)
    first = jnp.zeros((1, query_count), jnp.float32)
    for number in range(1, MOST_DOC + 1):
        smaller = jnp.where(docs < number, 1.0, 0.0)
        begins = jnp.sum(jnp.sum(smaller, axis=0, keepdims=True), axis=1, keepdims=True)
        first = jnp.where(begins <= place, jnp.maximum(first, begins), first)
    return first


def shift_of(chip, core):
    return jnp.where(core == 0, REACH - PAIR * chip, PAIR + PAIR * chip)


def pick_kernel(own_ref, held_ref, out_ref):
    own, tok = lax.axis_index("key"), lax.axis_index("tok")
    rows = held_ref.shape[0]
    takers = out_ref.shape[0] // PAIR
    swapped = (lax.rem(own, PAIR) == 0) & (shift_of(tok // CORES, lax.rem(tok, CORES)) == REACH)
    held = held_ref[...]
    for taker in range(takers):
        out_ref[taker] = held

    @pl.when(swapped)
    def _():
        begin = pl.multiple_of(lax.rem(tok, CORES) * rows, rows)
        half = pl.ds(begin, rows)
        pair = jnp.concatenate([own_ref[0, half, :], own_ref[1, half, :]], axis=1)
        for taker in range(takers):
            out_ref[takers + taker] = pair

    @pl.when(jnp.logical_not(swapped))
    def _():
        for taker in range(takers):
            out_ref[takers + taker] = held_ref[...]


def pick(own, held, taker_count):
    return pl.pallas_call(
        pick_kernel,
        out_shape=jax.ShapeDtypeStruct((taker_count,) + held.shape, jnp.bfloat16),
        in_specs=[VMEM, VMEM],
        out_specs=VMEM,
        compiler_params=pltpu.CompilerParams(vmem_limit_bytes=8 << 20),
        name="pick",
    )(own, held)


def mask_half(scores, own, core, first, blocks_shape, query_count):
    source_count, rows, _ = blocks_shape
    row = lax.broadcasted_iota(jnp.int32, (rows, query_count), 0).astype(jnp.float32)
    chips = source_count // PAIR
    pieces = []
    for source in range(source_count):
        parity, chip = source // chips, source % chips
        shift = shift_of(chip, core)
        if parity == 0:
            shift = jnp.where((lax.rem(own, PAIR) == 1) & (shift == REACH), 0, shift)
        number = own // PAIR * PAIR + parity - shift
        start = number * query_count + core * rows
        allowed = row >= first - start.astype(jnp.float32)
        pieces.append(jnp.where(allowed, scores[source * rows : (source + 1) * rows] * FACTOR, LOW))
    return pieces


def near_kernel(docs_ref, own_ref, blocks_ref, first_ref, stats_ref, sums_ref):
    own, core = lax.axis_index("key"), lax.rem(lax.axis_index("tok"), CORES)
    query_count = first_ref.shape[1]
    first = find_first(docs_ref, own, query_count)
    first_ref[...] = first
    blocks = blocks_ref[...].reshape(-1, 2 * HEAD_SIZE)
    queries = own_ref[2]
    scores = dot(blocks[:, :HEAD_SIZE], queries, ((1,), (1,)))
    pieces = mask_half(scores, own, core, first, blocks_ref.shape, query_count)
    scores = dot(own_ref[0], queries, ((1,), (1,)))
    row = lax.broadcasted_iota(jnp.int32, scores.shape, 0)
    lane = lax.broadcasted_iota(jnp.int32, scores.shape, 1)
    begin = first - (own * query_count).astype(jnp.float32)
    allowed = (row <= lane) & (row.astype(jnp.float32) >= begin)
    pieces.append(jnp.where(allowed, scores * FACTOR, LOW))
    scores = jnp.concatenate(pieces, axis=0)
    highest = jnp.max(scores, axis=0, keepdims=True)
    weights = jnp.exp2(scores - highest)
    stats_ref[0:1, :] = highest
    stats_ref[1:2, :] = jnp.sum(weights, axis=0, keepdims=True)
    values = jnp.concatenate([blocks[:, HEAD_SIZE:], own_ref[1]], axis=0)
    sums_ref[...] = dot(values, weights.astype(jnp.bfloat16), ((0,), (0,)))


def far_kernel(first_ref, own_ref, blocks_ref, stats_ref, sums_ref, out_ref):
    own, core = lax.axis_index("key"), lax.rem(lax.axis_index("tok"), CORES)
    query_count = first_ref.shape[1]
    blocks = blocks_ref[...].reshape(-1, 2 * HEAD_SIZE)
    scores = dot(blocks[:, :HEAD_SIZE], own_ref[2], ((1,), (1,)))
    pieces = mask_half(scores, own, 1 - core, first_ref[...], blocks_ref.shape, query_count)
    scores = jnp.concatenate(pieces, axis=0)
    before = stats_ref[0:1, :]
    highest = jnp.maximum(before, jnp.max(scores, axis=0, keepdims=True))
    weights = jnp.exp2(scores - highest)
    keep = jnp.exp2(before - highest)
    total = keep * stats_ref[1:2, :] + jnp.sum(weights, axis=0, keepdims=True)
    weighted = dot(blocks[:, HEAD_SIZE:], weights.astype(jnp.bfloat16), ((0,), (0,)))
    attn = ((keep * sums_ref[...] + weighted) * (1.0 / total)).astype(jnp.bfloat16)
    for target in range(out_ref.shape[0]):
        out_ref[target] = attn


def cost(query_count, key_count):
    scores = query_count * key_count
    return pl.CostEstimate(
        flops=4 * HEAD_SIZE * scores, transcendentals=scores, bytes_accessed=1 << 20
    )


def attend_near(docs, own, blocks):
    query_count = own.shape[1]
    return pl.pallas_call(
        near_kernel,
        out_shape=[
            jax.ShapeDtypeStruct((1, query_count), jnp.float32),
            jax.ShapeDtypeStruct((8, query_count), jnp.float32),
            jax.ShapeDtypeStruct((HEAD_SIZE, query_count), jnp.float32),
        ],
        in_specs=[VMEM] * 3,
        out_specs=[VMEM] * 3,
        compiler_params=pltpu.CompilerParams(vmem_limit_bytes=12 << 20),
        cost_estimate=cost(query_count, blocks.shape[0] * blocks.shape[1] + query_count),
        name="near",
    )(docs, own, blocks)


def attend_far(first, own, blocks, stats, sums, target_count):
    query_count = first.shape[1]
    return pl.pallas_call(
        far_kernel,
        out_shape=jax.ShapeDtypeStruct((target_count, HEAD_SIZE, query_count), jnp.bfloat16),
        in_specs=[VMEM] * 5,
        out_specs=VMEM,
        compiler_params=pltpu.CompilerParams(vmem_limit_bytes=12 << 20),
        cost_estimate=cost(query_count, blocks.shape[0] * blocks.shape[1]),
        name="far",
    )(first, own, blocks, stats, sums)


def sum_kernel(shares_ref, out_ref):
    total = shares_ref[0].astype(jnp.float32)
    for place in range(1, shares_ref.shape[0]):
        total += shares_ref[place].astype(jnp.float32)
    out_ref[...] = total.astype(jnp.bfloat16)


def sum_shares(shares):
    return pl.pallas_call(
        sum_kernel,
        out_shape=jax.ShapeDtypeStruct(shares.shape[1:], jnp.bfloat16),
        in_specs=[VMEM],
        out_specs=VMEM,
        compiler_params=pltpu.CompilerParams(vmem_limit_bytes=4 << 20),
        name="sum_shares",
    )(shares)


def exchange(x, axis, groups=None):
    return lax.all_to_all(x, axis, 0, 0, tiled=True, axis_index_groups=groups)


def per_device(queries, keys, values, doc_ids, out_weight):
    key_count, tok_count, kv_count = (lax.axis_size(name) for name in ("key", "tok", "kv"))
    row_count = queries.shape[0]
    chips = tok_count // CORES
    beside = [
        [(begin + parity) * tok_count + chip * CORES + core for parity in range(PAIR) for chip in range(chips)]
        for begin in range(0, key_count, PAIR)
        for core in range(CORES)
    ]
    shifts = [REACH - tok if tok % CORES == 0 else PAIR + tok - 1 for tok in range(tok_count)]
    later = [
        (begin * tok_count + tok, (begin + shifts[tok]) * tok_count + tok)
        for begin in range(key_count)
        for tok in range(tok_count)
        if begin + shifts[tok] < key_count
    ]
    half = start(keys, values)
    held = lax.ppermute(half, ("key", "tok"), later)
    own, docs = load(queries, keys, values, doc_ids.reshape(-1, LANES))
    blocks = exchange(pick(own, held, PAIR * chips), ("key", "tok"), beside)
    other_blocks = lax.ppermute(blocks, "tok", [(i, i ^ 1) for i in range(tok_count)])
    first, stats, sums = attend_near(docs, own, blocks)
    attn = attend_far(first, own, other_blocks, stats, sums, tok_count)
    attn = exchange(attn, "tok").reshape(tok_count * HEAD_SIZE, row_count)
    total = jnp.einsum("kq,kn->qn", attn, out_weight, preferred_element_type=jnp.float32)
    total = total.astype(jnp.bfloat16).reshape(kv_count, row_count // kv_count, -1)
    return sum_shares(exchange(total, "kv"))


def solution(mesh):
    placed = (P("key", ("kv", "tok")), P("key", "kv"), P("key", "kv"), P(), P("kv", "tok"))

    return jax.shard_map(
        per_device, mesh=mesh, in_specs=placed, out_specs=P(("key", "kv"), "tok"), check_vma=False
    )
```
